32 devices in a mesh: kpool: 8 (over y, x, core), band: 4 (over z).
Axes of the slice: x: 2, y: 2, z: 4, core: 2. Of those that a mesh axis runs over, the one named last changes fastest.
Arguments:
- psi: bfloat16 [8, 2, 4, 48, 2304], P('kpool', None, 'band'), may hold values from -6 to 6
- kpoint_of_pool: int32 [8], replicated, may hold values from 0 to 7, each once
Outputs:
- exchange: float32 [8, 2, 4, 48, 2304], P('kpool', None, 'band')
The draws below stay inside these ranges and needn't reach their ends.
Inputs may be any that keep to these rules, and one draw needn't show every extreme that they name: `kpoint_of_pool`: each value appears once.
All inputs are finite; a program needn't handle non-finite values.
Results may differ from the reference program's by a relative error of at most 0.0003.
Values may be sent and summed in bfloat16 or wider, within the bound.
A program may use at most 64 MiB of HBM per device.

```python
import jax
import jax.numpy as jnp
from jax import lax

GRID = 48
KMESH = 4
ROUNDS = 1
NK = 8
BLOCK = 4


def levels(stream_key, shape, split, smallest, top_value):
    def one(axis_at, parts):
        draws = jax.random.uniform(jax.random.fold_in(jax.random.fold_in(stream_key, 6), axis_at), (parts,), jnp.float32, smallest / len(split), top_value / len(split))
        return jnp.repeat(jnp.exp(draws), shape[axis_at] // parts).reshape((-1,) + (1,) * (len(shape) - axis_at - 1))

    loudness = one(*split[0])
    for cut in split[1:]:
        loudness = loudness * one(*cut)
    return loudness


def normal_values(stream_key, extent, deviation, limit, shards=(), kind=jnp.bfloat16):
    values = jax.random.normal(stream_key, extent, jnp.float32) * deviation
    if len(shards) > 0:
        values = levels(stream_key, extent, shards, -0.22, 0.18) * values
    return jnp.clip(values, min=-limit, max=limit).astype(kind)


def setup_inputs(seed: int = 0) -> dict:
    splits = jax.random.split(jax.random.key(seed), 3)
    psi = normal_values(splits[0], (NK, 2, BLOCK, GRID, GRID * GRID), 1.0, 6.0, ((0, 8), (2, 4)))
    kpoint_of_pool = jax.random.permutation(splits[1], NK).astype(jnp.int32)
    return {"psi": psi, "kpoint_of_pool": kpoint_of_pool}


def kpoint_coords(labels):
    first = labels % KMESH
    second = (labels // KMESH) % KMESH
    third = labels // (KMESH * KMESH)
    return jnp.stack([first, second, third], axis=1).astype(jnp.float32) / KMESH


def coulomb(offset):
    index = jnp.arange(GRID, dtype=jnp.int32)
    freq = jnp.where(index < GRID // 2, index, index - GRID).astype(jnp.float32)
    edge = index == GRID // 2
    along_x = (offset[0] + freq) ** 2
    along_y = (offset[1] + freq) ** 2
    along_z = (offset[2] + freq) ** 2
    squared = along_x[:, None, None] + along_y[None, :, None] + along_z[None, None, :]
    cutoff = edge[:, None, None] | edge[None, :, None] | edge[None, None, :]
    safe = jnp.where(cutoff, 1.0, squared)
    amplitude = GRID ** 1.5 / 16.0
    return jnp.where(cutoff, 0.0, amplitude / safe)


def reference(psi, kpoint_of_pool):
    orbitals = lax.complex(psi[:, 0].astype(jnp.float32), psi[:, 1].astype(jnp.float32))
    orbitals = orbitals.reshape(NK, BLOCK, GRID, GRID, GRID)
    coords = kpoint_coords(kpoint_of_pool)
    weight = -(2.0 * ROUNDS * BLOCK) ** -0.5
    npoints = GRID * GRID * GRID

    def one_pool(pool):
        own = orbitals[pool]
        total = jnp.zeros_like(own)
        for turn in range(1, ROUNDS + 1):
            for direction in (1, -1):
                partner = (pool - direction * turn) % NK
                other = orbitals[partner]
                kernel = coulomb(coords[pool] - coords[partner])
                density = jnp.conj(other)[None] * own[:, None]
                spectrum = jnp.fft.fftn(density, axes=(2, 3, 4)) / npoints
                potential = jnp.fft.ifftn(spectrum * kernel, axes=(2, 3, 4)) * npoints
                total = total + jnp.sum(other[None] * potential, axis=1)
        total = total * weight
        return jnp.stack([jnp.real(total), jnp.imag(total)]).reshape(2, BLOCK, GRID, GRID * GRID)

    return lax.map(one_pool, jnp.arange(NK, dtype=jnp.int32))
```

```python
import functools
import math

import jax
import jax.numpy as jnp
import numpy as np
from jax import lax
from jax.experimental import pallas as pl
from jax.experimental.pallas import tpu as pltpu
from jax.sharding import PartitionSpec as P

KMESH = 4
ROUNDS = 1


def passed_along(value, axis, by):
    size = lax.axis_size(axis)
    return lax.ppermute(value, axis, [(i, (i + by) % size) for i in range(size)])


def kpoint_coords(labels):
    first = labels % KMESH
    second = labels // KMESH % KMESH
    third = labels // (KMESH * KMESH)
    return jnp.stack([first, second, third], axis=1).astype(jnp.float32) / KMESH


def half_width(grid):
    return -(-grid // 64) * 64


def coulomb(offset, grid):
    half = half_width(grid)
    index = jnp.arange(grid, dtype=jnp.int32)
    lane = jnp.arange(2 * half, dtype=jnp.int32) % half

    def freq(i):
        return jnp.where(i < grid // 2, i, i - grid).astype(jnp.float32)

    edge = index == grid // 2
    edge_z = (lane == grid // 2) | (lane >= grid)
    along_x = (offset[0] + freq(index)) ** 2
    along_y = (offset[1] + freq(index)) ** 2
    along_z = (offset[2] + freq(lane)) ** 2
    squared = along_x[None, :, None] + along_y[:, None, None] + along_z[None, None, :]
    cutoff = edge[None, :, None] | edge[:, None, None] | edge_z[None, None, :]
    safe = jnp.where(cutoff, 1.0, squared)
    amplitude = grid**1.5 / 16.0
    return jnp.where(cutoff, 0.0, amplitude / safe) / (grid * grid * grid)


def two_parts(table):
    high = table.astype(jnp.bfloat16)
    low = (table - high.astype(np.float32)).astype(jnp.bfloat16)
    return high, low


def dft_tables(grid):
    half = half_width(grid)
    index = np.arange(grid)
    angles = (index[:, None] * index[None, :] % grid) * (2.0 * math.pi / grid)
    cosine = np.cos(angles).astype(np.float32)
    sine = np.sin(angles).astype(np.float32)
    lanes = []
    for sign in (1.0, -1.0):
        full = np.zeros((2 * half, 2 * half), np.float32)
        full[:grid, :grid] = cosine
        full[half : half + grid, half : half + grid] = cosine
        full[:grid, half : half + grid] = -sign * sine
        full[half : half + grid, :grid] = sign * sine
        high, low = two_parts(full)
        lanes.append(np.block([[high, low], [high, np.zeros_like(low)]]))
    high, low = two_parts(np.concatenate([cosine, sine], axis=0))
    rows = np.concatenate([high, high, low], axis=1)
    return np.stack(lanes), rows


def split(x):
    high = x.astype(jnp.bfloat16)
    low = (x - high.astype(jnp.float32)).astype(jnp.bfloat16)
    return high, low


def kernel(grid, batch, own_ref, band_ref, v_ref, lanes_ref, rows_ref, acc_ref, back_ref, field):
    half = half_width(grid)
    width = 2 * half
    first = lax.broadcasted_iota(jnp.int32, (1, width), 1) < half
    sign = jnp.where(first, 1.0, -1.0).astype(jnp.float32)

    def swap(x):
        return pltpu.roll(x, half, 1)

    def turned(x):
        return swap(x) * sign

    def both(x):
        other = swap(x)
        return jnp.where(first, x, other), jnp.where(first, other, x)

    def along_lanes(x, which):
        high, low = split(x)
        out = jnp.dot(
            jnp.concatenate([high, low], axis=1),
            lanes_ref[which],
            preferred_element_type=jnp.float32,
        )
        return out[:, :width] + out[:, width:]

    def along_rows(xs, sense):
        parts = []
        for x in xs:
            high, low = split(x)
            parts.append(jnp.concatenate([high, low, high], axis=0))
        outs = []
        for at in range(0, len(parts), 2):
            pair = jnp.concatenate(parts[at : at + 2], axis=1)
            out = jnp.dot(rows_ref[...], pair, preferred_element_type=jnp.float32)
            for j in range(len(parts[at : at + 2])):
                piece = out[:, j * width : (j + 1) * width]
                q = turned(piece[grid:])
                outs.append(piece[:grid] + q if sense > 0 else piece[:grid] - q)
        return outs

    def rows_of(step):
        return pl.ds(pl.multiple_of(step * (batch * grid), batch * grid), batch * grid)

    def forward(step, carry):
        rows = rows_of(step)
        own = own_ref[rows, :].astype(jnp.float32)
        b_re, b_im = both(band_ref[0, rows, :].astype(jnp.float32))
        dens = b_re * own + b_im * turned(own)
        spec = along_lanes(dens, 0)
        outs = along_rows([spec[j * grid : (j + 1) * grid] for j in range(batch)], 1)
        field[rows, :] = jnp.concatenate(outs, axis=0)
        return carry

    lax.fori_loop(0, grid // batch, forward, 0)

    def middle(step, carry):
        at = step * batch
        xs = [field[pl.ds(at + j, grid, stride=grid), :] for j in range(batch)]
        spec = along_rows(xs, 1)
        spec = [spec[j] * v_ref[at + j] for j in range(batch)]
        outs = along_rows(spec, -1)
        for j in range(batch):
            field[pl.ds(at + j, grid, stride=grid), :] = outs[j]
        return carry

    lax.fori_loop(0, grid // batch, middle, 0)

    fresh = pl.program_id(0) == 0

    def backward(step, carry):
        rows = rows_of(step)
        mid = field[rows, :]
        outs = along_rows([mid[j * grid : (j + 1) * grid] for j in range(batch)], -1)
        pot = along_lanes(jnp.concatenate(outs, axis=0), 1)
        own = own_ref[rows, :].astype(jnp.float32)
        b_re, b_im = both(band_ref[0, rows, :].astype(jnp.float32))
        w_re, w_im = both(pot)
        back_ref[0, rows, :] = w_re * own + w_im * turned(own)
        new = b_re * pot - b_im * turned(pot)
        acc_ref[rows, :] = jnp.where(fresh, new, acc_ref[rows, :] + new)
        return carry

    lax.fori_loop(0, grid // batch, backward, 0)


def pair_sums(own, bands, v, grid, batch=8):
    count = bands.shape[0]
    points, width = own.shape
    lanes, rows = dft_tables(grid)
    whole = pl.BlockSpec(memory_space=pltpu.VMEM)
    return pl.pallas_call(
        functools.partial(kernel, grid, batch),
        grid=(count,),
        in_specs=[
            whole,
            pl.BlockSpec((1, points, width), lambda m: (m, 0, 0)),
            whole,
            whole,
            whole,
        ],
        out_specs=[
            pl.BlockSpec((points, width), lambda m: (0, 0)),
            pl.BlockSpec((1, points, width), lambda m: (m, 0, 0)),
        ],
        out_shape=[
            jax.ShapeDtypeStruct((points, width), jnp.float32),
            jax.ShapeDtypeStruct((count, points, width), jnp.float32),
        ],
        scratch_shapes=[pltpu.VMEM((points, width), jnp.float32)],
        compiler_params=pltpu.CompilerParams(dimension_semantics=("arbitrary",)),
    )(own, bands, v, jnp.asarray(lanes), jnp.asarray(rows))


def per_device(psi, kpoint_of_pool):
    own = psi[0]
    grid = own.shape[2]
    half = half_width(grid)
    band_dev = own.shape[1]
    block = band_dev * lax.axis_size("band")
    pools = lax.axis_size("kpool")
    myself = lax.axis_index("kpool")
    coords = kpoint_coords(kpoint_of_pool)
    here = lax.dynamic_index_in_dim(coords, myself, 0, keepdims=False)
    there = lax.dynamic_index_in_dim(coords, (myself - 1) % pools, 0, keepdims=False)
    v = coulomb(here - there, grid)
    points = grid * grid
    parts = own.reshape(2, band_dev, points, grid)
    parts = jnp.pad(parts, ((0, 0), (0, 0), (0, 0), (0, half - grid)))
    packed = jnp.concatenate([parts[0], parts[1]], axis=-1)
    arrived = passed_along(packed, "kpool", 1)
    bands = lax.all_gather(arrived, "band", axis=0, tiled=True)
    accs, back = [], None
    for n in range(band_dev):
        acc, rows = pair_sums(packed[n], bands, v, grid)
        accs.append(acc)
        back = rows if back is None else back + rows
    shares = lax.psum_scatter(back, "band", scatter_dimension=0, tiled=True)
    returned = passed_along(shares, "kpool", -1)
    weight = -((2.0 * ROUNDS * block) ** (-0.5))
    total = (jnp.stack(accs) + returned) * weight
    result = jnp.stack([total[..., :grid], total[..., half : half + grid]])
    return result.reshape(2, band_dev, grid, grid * grid)[None]


def solution(mesh):
    in_specs = (P("kpool", None, "band", None, None), P())
    out_specs = P("kpool", None, "band", None, None)
    return jax.shard_map(
        per_device, mesh=mesh, in_specs=in_specs, out_specs=out_specs, check_vma=False
    )
```

```python
import functools
import math

import jax
import jax.numpy as jnp
import numpy as np
from jax import lax
from jax.experimental import pallas as pl
from jax.experimental.pallas import tpu as pltpu
from jax.sharding import PartitionSpec as P

KMESH = 4
ROUNDS = 1
RETURNED = 2


def kpoint_coords(labels):
    first = labels % KMESH
    second = labels // KMESH % KMESH
    third = labels // (KMESH * KMESH)
    return jnp.stack([first, second, third], axis=1).astype(jnp.float32) / KMESH


def half_width(grid):
    return -(-grid // 64) * 64


def coulomb(offset, grid):
    half = half_width(grid)
    index = jnp.arange(grid, dtype=jnp.int32)
    lane = jnp.arange(2 * half, dtype=jnp.int32) % half

    def freq(i):
        return jnp.where(i < grid // 2, i, i - grid).astype(jnp.float32)

    edge = index == grid // 2
    edge_z = (lane == grid // 2) | (lane >= grid)
    along_x = (offset[0] + freq(index)) ** 2
    along_y = (offset[1] + freq(index)) ** 2
    along_z = (offset[2] + freq(lane)) ** 2
    squared = along_x[None, :, None] + along_y[:, None, None] + along_z[None, None, :]
    cutoff = edge[None, :, None] | edge[:, None, None] | edge_z[None, None, :]
    safe = jnp.where(cutoff, 1.0, squared)
    amplitude = grid**1.5 / 16.0
    return jnp.where(cutoff, 0.0, amplitude / safe) / (grid * grid * grid)


def two_parts(table):
    high = table.astype(jnp.bfloat16)
    low = (table - high.astype(np.float32)).astype(jnp.bfloat16)
    return high, low


def dft_tables(grid):
    half = half_width(grid)
    index = np.arange(grid)
    angles = (index[:, None] * index[None, :] % grid) * (2.0 * math.pi / grid)
    cosine = np.cos(angles).astype(np.float32)
    sine = np.sin(angles).astype(np.float32)
    lanes = []
    for sign in (1.0, -1.0):
        full = np.zeros((2 * half, 2 * half), np.float32)
        full[:grid, :grid] = cosine
        full[half : half + grid, half : half + grid] = cosine
        full[:grid, half : half + grid] = -sign * sine
        full[half : half + grid, :grid] = sign * sine
        high, low = two_parts(full)
        lanes.append(np.block([[high, low], [high, np.zeros_like(low)]]))
    high, low = two_parts(np.concatenate([cosine, sine], axis=0))
    rows = np.concatenate([high, high, low], axis=1)
    return np.stack(lanes), rows


def split(x):
    high = x.astype(jnp.bfloat16)
    low = (x - high.astype(jnp.float32)).astype(jnp.bfloat16)
    return high, low


def kernel(grid, batch, started, own_ref, band_ref, v_ref, lanes_ref, rows_ref, *refs):
    acc_in = refs[0] if started else None
    field = refs[-1]
    acc_ref, back_ref = (refs[1 if started else 0 :][:-1] + (None,))[:2]
    half = half_width(grid)
    width = 2 * half
    first = lax.broadcasted_iota(jnp.int32, (1, width), 1) < half
    sign = jnp.where(first, 1.0, -1.0).astype(jnp.float32)

    def swap(x):
        return pltpu.roll(x, half, 1)

    def turned(x):
        return swap(x) * sign

    def both(x):
        other = swap(x)
        return jnp.where(first, x, other), jnp.where(first, other, x)

    def along_lanes(x, which):
        high, low = split(x)
        out = jnp.dot(
            jnp.concatenate([high, low], axis=1),
            lanes_ref[which],
            preferred_element_type=jnp.float32,
        )
        return out[:, :width] + out[:, width:]

    def along_rows(xs, sense):
        parts = []
        for x in xs:
            high, low = split(x)
            parts.append(jnp.concatenate([high, low, high], axis=0))
        outs = []
        for at in range(0, len(parts), 2):
            pair = jnp.concatenate(parts[at : at + 2], axis=1)
            out = jnp.dot(rows_ref[...], pair, preferred_element_type=jnp.float32)
            for j in range(len(parts[at : at + 2])):
                piece = out[:, j * width : (j + 1) * width]
                q = turned(piece[grid:])
                outs.append(piece[:grid] + q if sense > 0 else piece[:grid] - q)
        return outs

    def rows_of(step):
        return pl.ds(pl.multiple_of(step * (batch * grid), batch * grid), batch * grid)

    def forward(step, carry):
        rows = rows_of(step)
        own = own_ref[rows, :].astype(jnp.float32)
        b_re, b_im = both(band_ref[rows, :].astype(jnp.float32))
        dens = b_re * own + b_im * turned(own)
        spec = along_lanes(dens, 0)
        outs = along_rows([spec[j * grid : (j + 1) * grid] for j in range(batch)], 1)
        field[rows, :] = jnp.concatenate(outs, axis=0)
        return carry

    lax.fori_loop(0, grid // batch, forward, 0)

    def middle(step, carry):
        at = step * batch
        xs = [field[pl.ds(at + j, grid, stride=grid), :] for j in range(batch)]
        spec = along_rows(xs, 1)
        spec = [spec[j] * v_ref[at + j] for j in range(batch)]
        outs = along_rows(spec, -1)
        for j in range(batch):
            field[pl.ds(at + j, grid, stride=grid), :] = outs[j]
        return carry

    lax.fori_loop(0, grid // batch, middle, 0)

    def backward(step, carry):
        rows = rows_of(step)
        mid = field[rows, :]
        outs = along_rows([mid[j * grid : (j + 1) * grid] for j in range(batch)], -1)
        pot = along_lanes(jnp.concatenate(outs, axis=0), 1)
        b_re, b_im = both(band_ref[rows, :].astype(jnp.float32))
        if back_ref is not None:
            own = own_ref[rows, :].astype(jnp.float32)
            w_re, w_im = both(pot)
            back_ref[rows, :] = w_re * own + w_im * turned(own)
        new = b_re * pot - b_im * turned(pot)
        acc_ref[rows, :] = acc_in[rows, :] + new if started else new
        return carry

    lax.fori_loop(0, grid // batch, backward, 0)


def pair_sums(own, band, v, acc, with_back, grid, batch=8):
    points, width = own.shape
    lanes, rows = dft_tables(grid)
    whole = pl.BlockSpec(memory_space=pltpu.VMEM)
    args = [own, band, v, jnp.asarray(lanes), jnp.asarray(rows)]
    if acc is not None:
        args.append(acc)
    field = jax.ShapeDtypeStruct((points, width), jnp.float32)
    outs = 2 if with_back else 1
    return pl.pallas_call(
        functools.partial(kernel, grid, batch, acc is not None),
        in_specs=[whole] * len(args),
        out_specs=[whole] * outs,
        out_shape=[field] * outs,
        input_output_aliases={} if acc is None else {5: 0},
        scratch_shapes=[pltpu.VMEM((points, width), jnp.float32)],
        cost_estimate=pl.CostEstimate(
            flops=10**10, bytes_accessed=16 * points * width, transcendentals=0
        ),
    )(*args)


def sent(value, pools_by, bands_by):
    pools, bands = lax.axis_size("kpool"), lax.axis_size("band")
    pairs = [
        (p * bands + n, (p + pools_by) % pools * bands + (n + bands_by) % bands)
        for p in range(pools)
        for n in range(bands)
    ]
    return lax.ppermute(value, ("kpool", "band"), pairs)


def per_device(psi, kpoint_of_pool):
    own = psi[0]
    grid = own.shape[2]
    half = half_width(grid)
    band_dev = own.shape[1]
    ring = lax.axis_size("band")
    block = band_dev * ring
    pools = lax.axis_size("kpool")
    myself = lax.axis_index("kpool")
    coords = kpoint_coords(kpoint_of_pool)
    here = lax.dynamic_index_in_dim(coords, myself, 0, keepdims=False)
    lower = lax.dynamic_index_in_dim(coords, (myself - 1) % pools, 0, keepdims=False)
    upper = lax.dynamic_index_in_dim(coords, (myself + 1) % pools, 0, keepdims=False)
    v_lower = coulomb(here - lower, grid)
    v_upper = coulomb(here - upper, grid)
    points = grid * grid
    parts = own.reshape(2, band_dev, points, grid)
    parts = jnp.pad(parts, ((0, 0), (0, 0), (0, 0), (0, half - grid)))
    packed = jnp.concatenate([parts[0], parts[1]], axis=-1)

    returning = [step for step in range(ring) if step < RETURNED]
    absent = [-step % ring for step in returning]
    accs = [None] * band_dev
    returned = []
    moving = packed
    for step in range(ring):
        sides = [(sent(moving, 1, 0), v_lower, step in returning)]
        if step not in absent:
            sides.append((sent(moving, -1, 0), v_upper, False))
        if step + 1 < ring:
            moving = sent(moving, 0, 1)
        for bands, v, with_back in sides:
            back = [None] * band_dev
            for n in range(band_dev):
                for m in range(band_dev):
                    outs = pair_sums(packed[n], bands[m], v, accs[n], with_back, grid)
                    accs[n] = outs[0]
                    if with_back:
                        back[m] = outs[1] if back[m] is None else back[m] + outs[1]
            if with_back:
                returned.append(sent(jnp.stack(back), -1, -step))
    weight = -((2.0 * ROUNDS * block) ** (-0.5))
    total = jnp.stack(accs)
    for rows in returned:
        total = total + rows
    total = total * weight
    result = jnp.stack([total[..., :grid], total[..., half : half + grid]])
    return result.reshape(2, band_dev, grid, grid * grid)[None]


def solution(mesh):
    in_specs = (P("kpool", None, "band", None, None), P())
    out_specs = P("kpool", None, "band", None, None)
    return jax.shard_map(
        per_device, mesh=mesh, in_specs=in_specs, out_specs=out_specs, check_vma=False
    )
```

```python
import functools
import math

import jax
import jax.numpy as jnp
import numpy as np
from jax import lax
from jax.experimental import pallas as pl
from jax.experimental.pallas import tpu as pltpu
from jax.sharding import PartitionSpec as P

KMESH = 4
ROUNDS = 1


def kpoint_coords(labels):
    first = labels % KMESH
    second = labels // KMESH % KMESH
    third = labels // (KMESH * KMESH)
    return jnp.stack([first, second, third], axis=1).astype(jnp.float32) / KMESH


def half_width(grid):
    return -(-grid // 64) * 64


def coulomb(offset, grid):
    half = half_width(grid)
    index = jnp.arange(grid, dtype=jnp.int32)
    lane = jnp.arange(2 * half, dtype=jnp.int32) % half

    def freq(i):
        return jnp.where(i < grid // 2, i, i - grid).astype(jnp.float32)

    edge = index == grid // 2
    edge_z = (lane == grid // 2) | (lane >= grid)
    along_x = (offset[0] + freq(index)) ** 2
    along_y = (offset[1] + freq(index)) ** 2
    along_z = (offset[2] + freq(lane)) ** 2
    squared = along_x[None, :, None] + along_y[:, None, None] + along_z[None, None, :]
    cutoff = edge[None, :, None] | edge[:, None, None] | edge_z[None, None, :]
    safe = jnp.where(cutoff, 1.0, squared)
    amplitude = grid**1.5 / 16.0
    return jnp.where(cutoff, 0.0, amplitude / safe) / (grid * grid * grid)


def two_parts(table):
    high = table.astype(jnp.bfloat16)
    low = (table - high.astype(np.float32)).astype(jnp.bfloat16)
    return high, low


def dft_tables(grid):
    half = half_width(grid)
    index = np.arange(grid)
    angles = (index[:, None] * index[None, :] % grid) * (2.0 * math.pi / grid)
    cosine = np.cos(angles).astype(np.float32)
    sine = np.sin(angles).astype(np.float32)
    lanes = []
    for sign in (1.0, -1.0):
        full = np.zeros((2 * half, 2 * half), np.float32)
        full[:grid, :grid] = cosine
        full[half : half + grid, half : half + grid] = cosine
        full[:grid, half : half + grid] = -sign * sine
        full[half : half + grid, :grid] = sign * sine
        high, low = two_parts(full)
        lanes.append(np.block([[high, low], [high, np.zeros_like(low)]]))
    high, low = two_parts(np.concatenate([cosine, sine], axis=0))
    rows = np.concatenate([high, high, low], axis=1)
    return np.stack(lanes), rows


def split(x):
    high = x.astype(jnp.bfloat16)
    low = (x - high.astype(jnp.float32)).astype(jnp.bfloat16)
    return high, low


def kernel(grid, batch, sides, started, with_back, *refs):
    own_ref, refs = refs[0], refs[1:]
    band_refs, refs = refs[: len(sides)], refs[len(sides) :]
    v_refs, refs = refs[: max(sides) + 1], refs[max(sides) + 1 :]
    (lanes_ref, rows_ref), refs = refs[:2], refs[2:]
    acc_in = refs[0] if started else None
    acc_ref = refs[1 if started else 0]
    field = refs[-1]
    back_ref = refs[-2] if with_back else None
    half = half_width(grid)
    width = 2 * half
    first = lax.broadcasted_iota(jnp.int32, (1, width), 1) < half
    sign = jnp.where(first, 1.0, -1.0).astype(jnp.float32)

    def swap(x):
        return pltpu.roll(x, half, 1)

    def turned(x):
        return swap(x) * sign

    def both(x):
        other = swap(x)
        return jnp.where(first, x, other), jnp.where(first, other, x)

    def along_lanes(x, which):
        high, low = split(x)
        out = jnp.dot(
            jnp.concatenate([high, low], axis=1),
            lanes_ref[which],
            preferred_element_type=jnp.float32,
        )
        return out[:, :width] + out[:, width:]

    def along_rows(xs, sense):
        parts = []
        for x in xs:
            high, low = split(x)
            parts.append(jnp.concatenate([high, low, high], axis=0))
        outs = []
        for at in range(0, len(parts), 2):
            pair = jnp.concatenate(parts[at : at + 2], axis=1)
            out = jnp.dot(rows_ref[...], pair, preferred_element_type=jnp.float32)
            for j in range(len(parts[at : at + 2])):
                piece = out[:, j * width : (j + 1) * width]
                q = turned(piece[grid:])
                outs.append(piece[:grid] + q if sense > 0 else piece[:grid] - q)
        return outs

    def rows_of(step):
        return pl.ds(pl.multiple_of(step * (batch * grid), batch * grid), batch * grid)

    def one_pair(band_ref, v_ref, before):
        def forward(step, carry):
            rows = rows_of(step)
            own = own_ref[rows, :].astype(jnp.float32)
            b_re, b_im = both(band_ref[rows, :].astype(jnp.float32))
            dens = b_re * own + b_im * turned(own)
            spec = along_lanes(dens, 0)
            outs = along_rows([spec[j * grid : (j + 1) * grid] for j in range(batch)], 1)
            field[rows, :] = jnp.concatenate(outs, axis=0)
            return carry

        lax.fori_loop(0, grid // batch, forward, 0)

        def middle(step, carry):
            at = step * batch
            xs = [field[pl.ds(at + j, grid, stride=grid), :] for j in range(batch)]
            spec = along_rows(xs, 1)
            spec = [spec[j] * v_ref[at + j] for j in range(batch)]
            outs = along_rows(spec, -1)
            for j in range(batch):
                field[pl.ds(at + j, grid, stride=grid), :] = outs[j]
            return carry

        lax.fori_loop(0, grid // batch, middle, 0)

        def backward(step, carry):
            rows = rows_of(step)
            mid = field[rows, :]
            outs = along_rows([mid[j * grid : (j + 1) * grid] for j in range(batch)], -1)
            pot = along_lanes(jnp.concatenate(outs, axis=0), 1)
            b_re, b_im = both(band_ref[rows, :].astype(jnp.float32))
            if back_ref is not None:
                own = own_ref[rows, :].astype(jnp.float32)
                w_re, w_im = both(pot)
                back_ref[rows, :] = w_re * own + w_im * turned(own)
            new = b_re * pot - b_im * turned(pot)
            acc_ref[rows, :] = before[rows, :] + new if before is not None else new
            return carry

        lax.fori_loop(0, grid // batch, backward, 0)

    for at, side in enumerate(sides):
        one_pair(band_refs[at], v_refs[side], acc_ref if at > 0 else acc_in)


def pair_sums(own, bands, sides, vs, acc, with_back, grid, batch=8):
    points, width = own.shape
    lanes, rows = dft_tables(grid)
    whole = pl.BlockSpec(memory_space=pltpu.VMEM)
    low = min(sides)
    vs, sides = vs[low : max(sides) + 1], tuple(side - low for side in sides)
    args = [own, *bands, *vs, jnp.asarray(lanes), jnp.asarray(rows)]
    if acc is not None:
        args.append(acc)
    field = jax.ShapeDtypeStruct((points, width), jnp.float32)
    outs = 2 if with_back else 1
    return pl.pallas_call(
        functools.partial(kernel, grid, batch, sides, acc is not None, with_back),
        in_specs=[whole] * len(args),
        out_specs=[whole] * outs,
        out_shape=[field] * outs,
        input_output_aliases={} if acc is None else {len(args) - 1: 0},
        scratch_shapes=[pltpu.VMEM((points, width), jnp.float32)],
        cost_estimate=pl.CostEstimate(
            flops=len(bands) * 10**10, bytes_accessed=16 * points * width, transcendentals=0
        ),
    )(*args)


def sent(value, pools_by, bands_by):
    pools, bands = lax.axis_size("kpool"), lax.axis_size("band")
    pairs = [
        (p * bands + n, (p + pools_by) % pools * bands + (n + bands_by) % bands)
        for p in range(pools)
        for n in range(bands)
    ]
    return lax.ppermute(value, ("kpool", "band"), pairs)


def per_device(psi, kpoint_of_pool):
    own = psi[0]
    grid = own.shape[2]
    half = half_width(grid)
    band_dev = own.shape[1]
    ring = lax.axis_size("band")
    block = band_dev * ring
    pools = lax.axis_size("kpool")
    myself = lax.axis_index("kpool")
    coords = kpoint_coords(kpoint_of_pool)
    here = lax.dynamic_index_in_dim(coords, myself, 0, keepdims=False)
    lower = lax.dynamic_index_in_dim(coords, (myself - 1) % pools, 0, keepdims=False)
    upper = lax.dynamic_index_in_dim(coords, (myself + 1) % pools, 0, keepdims=False)
    v_lower = coulomb(here - lower, grid)
    v_upper = coulomb(here - upper, grid)
    points = grid * grid
    parts = own.reshape(2, band_dev, points, grid)
    parts = jnp.pad(parts, ((0, 0), (0, 0), (0, 0), (0, half - grid)))
    packed = jnp.concatenate([parts[0], parts[1]], axis=-1)

    held = {0: packed}
    for step in range(1, ring):
        if step > 1 and step == ring - 1:
            held[step] = sent(packed, 0, -1)
        else:
            held[step] = sent(held[step - 1], 0, 1)
    order = [(0, 0)]
    if ring > 1:
        order += [(0, 1)] + [(1, s) for s in range(1, ring - 1)][:1]
    late = [(0, s) for s in range(ring - 1, 1, -1)] + [(1, s) for s in range(2, ring - 1)]
    groups = [[pair] for pair in order] + ([late] if late else [])
    accs = [None] * band_dev
    returned = []
    vs = (v_lower, v_upper)
    for group in groups:
        with_back = group[0] in ((0, 0), (0, 1))
        arrived = [sent(held[step], 1 if side == 0 else -1, 0) for side, step in group]
        back = [None] * band_dev
        for n in range(band_dev):
            for m in range(band_dev):
                outs = pair_sums(
                    packed[n],
                    [bands[m] for bands in arrived],
                    tuple(side for side, _ in group),
                    vs,
                    accs[n],
                    with_back,
                    grid,
                )
                accs[n] = outs[0]
                if with_back:
                    back[m] = outs[1] if back[m] is None else back[m] + outs[1]
        if with_back:
            returned.append(sent(jnp.stack(back), -1, -group[0][1]))
    weight = -((2.0 * ROUNDS * block) ** (-0.5))
    total = jnp.stack(accs)
    for rows in returned:
        total = total + rows
    total = total * weight
    result = jnp.stack([total[..., :grid], total[..., half : half + grid]])
    return result.reshape(2, band_dev, grid, grid * grid)[None]


def solution(mesh):
    in_specs = (P("kpool", None, "band", None, None), P())
    out_specs = P("kpool", None, "band", None, None)
    return jax.shard_map(
        per_device, mesh=mesh, in_specs=in_specs, out_specs=out_specs, check_vma=False
    )
```

```python
import functools
import math

import jax
import jax.numpy as jnp
import numpy as np
from jax import lax
from jax.experimental import pallas as pl
from jax.experimental.pallas import tpu as pltpu
from jax.sharding import PartitionSpec as P

KMESH = 4
ROUNDS = 1


def kpoint_coords(labels):
    first = labels % KMESH
    second = labels // KMESH % KMESH
    third = labels // (KMESH * KMESH)
    return jnp.stack([first, second, third], axis=1).astype(jnp.float32) / KMESH


def half_width(grid):
    return -(-grid // 64) * 64


def coulomb(offset, grid):
    half = half_width(grid)
    index = jnp.arange(grid, dtype=jnp.int32)
    lane = jnp.arange(2 * half, dtype=jnp.int32) % half

    def freq(i):
        return jnp.where(i < grid // 2, i, i - grid).astype(jnp.float32)

    edge = index == grid // 2
    edge_z = (lane == grid // 2) | (lane >= grid)
    along_x = (offset[0] + freq(index)) ** 2
    along_y = (offset[1] + freq(index)) ** 2
    along_z = (offset[2] + freq(lane)) ** 2
    squared = along_x[None, :, None] + along_y[:, None, None] + along_z[None, None, :]
    cutoff = edge[None, :, None] | edge[:, None, None] | edge_z[None, None, :]
    safe = jnp.where(cutoff, 1.0, squared)
    amplitude = grid**1.5 / 16.0
    return jnp.where(cutoff, 0.0, amplitude / safe) / (grid * grid * grid)


def two_parts(table):
    high = table.astype(jnp.bfloat16)
    low = (table - high.astype(np.float32)).astype(jnp.bfloat16)
    return high, low


def dft_tables(grid):
    half = half_width(grid)
    index = np.arange(grid)
    angles = (index[:, None] * index[None, :] % grid) * (2.0 * math.pi / grid)
    cosine = np.cos(angles).astype(np.float32)
    sine = np.sin(angles).astype(np.float32)
    lanes = []
    for sign in (1.0, -1.0):
        full = np.zeros((2 * half, 2 * half), np.float32)
        full[:grid, :grid] = cosine
        full[half : half + grid, half : half + grid] = cosine
        full[:grid, half : half + grid] = -sign * sine
        full[half : half + grid, :grid] = sign * sine
        high, low = two_parts(full)
        lanes.append(np.block([[high, low], [high, np.zeros_like(low)]]))
    high, low = two_parts(np.concatenate([cosine, sine], axis=0))
    rows = np.concatenate([high, high, low], axis=1)
    return np.stack(lanes), rows


def split(x):
    high = x.astype(jnp.bfloat16)
    low = (x - high.astype(jnp.float32)).astype(jnp.bfloat16)
    return high, low


def kernel(grid, batch, count, started, *refs):
    own_ref, band_refs, v_refs = refs[0], refs[1 : 1 + count], refs[1 + count : 1 + 2 * count]
    lanes_ref, rows_ref = refs[1 + 2 * count : 3 + 2 * count]
    acc_in = refs[3 + 2 * count] if started else None
    acc_ref, field = refs[-2:]
    half = half_width(grid)
    width = 2 * half
    first = lax.broadcasted_iota(jnp.int32, (1, width), 1) < half
    sign = jnp.where(first, 1.0, -1.0).astype(jnp.float32)

    def swap(x):
        return pltpu.roll(x, half, 1)

    def turned(x):
        return swap(x) * sign

    def both(x):
        other = swap(x)
        return jnp.where(first, x, other), jnp.where(first, other, x)

    def along_lanes(x, which):
        high, low = split(x)
        out = jnp.dot(
            jnp.concatenate([high, low], axis=1),
            lanes_ref[which],
            preferred_element_type=jnp.float32,
        )
        return out[:, :width] + out[:, width:]

    def along_rows(xs, sense):
        parts = []
        for x in xs:
            high, low = split(x)
            parts.append(jnp.concatenate([high, low, high], axis=0))
        outs = []
        for at in range(0, len(parts), 2):
            pair = jnp.concatenate(parts[at : at + 2], axis=1)
            out = jnp.dot(rows_ref[...], pair, preferred_element_type=jnp.float32)
            for j in range(len(parts[at : at + 2])):
                piece = out[:, j * width : (j + 1) * width]
                q = turned(piece[grid:])
                outs.append(piece[:grid] + q if sense > 0 else piece[:grid] - q)
        return outs

    def rows_of(step):
        return pl.ds(pl.multiple_of(step * (batch * grid), batch * grid), batch * grid)

    def one_pair(band_ref, v_ref, before):
        def forward(step, carry):
            rows = rows_of(step)
            own = own_ref[rows, :].astype(jnp.float32)
            b_re, b_im = both(band_ref[rows, :].astype(jnp.float32))
            dens = b_re * own + b_im * turned(own)
            spec = along_lanes(dens, 0)
            outs = along_rows([spec[j * grid : (j + 1) * grid] for j in range(batch)], 1)
            field[rows, :] = jnp.concatenate(outs, axis=0)
            return carry

        lax.fori_loop(0, grid // batch, forward, 0)

        def middle(step, carry):
            at = step * batch
            xs = [field[pl.ds(at + j, grid, stride=grid), :] for j in range(batch)]
            spec = along_rows(xs, 1)
            spec = [spec[j] * v_ref[at + j] for j in range(batch)]
            outs = along_rows(spec, -1)
            for j in range(batch):
                field[pl.ds(at + j, grid, stride=grid), :] = outs[j]
            return carry

        lax.fori_loop(0, grid // batch, middle, 0)

        def backward(step, carry):
            rows = rows_of(step)
            mid = field[rows, :]
            outs = along_rows([mid[j * grid : (j + 1) * grid] for j in range(batch)], -1)
            pot = along_lanes(jnp.concatenate(outs, axis=0), 1)
            b_re, b_im = both(band_ref[rows, :].astype(jnp.float32))
            new = b_re * pot - b_im * turned(pot)
            acc_ref[rows, :] = before[rows, :] + new if before is not None else new
            return carry

        lax.fori_loop(0, grid // batch, backward, 0)

    for at in range(count):
        one_pair(band_refs[at], v_refs[at], acc_ref if at > 0 else acc_in)


def pair_sums(own, bands, vs, acc, grid):
    points, width = own.shape
    batch = grid // 2 if acc is None and grid % 2 == 0 else grid
    lanes, rows = dft_tables(grid)
    whole = pl.BlockSpec(memory_space=pltpu.VMEM)
    args = [own, *bands, *vs, jnp.asarray(lanes), jnp.asarray(rows)]
    if acc is not None:
        args.append(acc)
    return pl.pallas_call(
        functools.partial(kernel, grid, batch, len(bands), acc is not None),
        in_specs=[whole] * len(args),
        out_specs=whole,
        out_shape=jax.ShapeDtypeStruct((points, width), jnp.float32),
        input_output_aliases={} if acc is None else {len(args) - 1: 0},
        scratch_shapes=[pltpu.VMEM((points, width), jnp.float32)],
        cost_estimate=pl.CostEstimate(
            flops=len(bands) * 6 * 10**9, bytes_accessed=16 * points * width, transcendentals=0
        ),
    )(*args)


def sent(value, pools_by, bands_by):
    pools, bands = lax.axis_size("kpool"), lax.axis_size("band")
    pairs = [
        (p * bands + n, (p + pools_by) % pools * bands + (n + bands_by) % bands)
        for p in range(pools)
        for n in range(bands)
    ]
    return lax.ppermute(value, ("kpool", "band"), pairs)


def per_device(psi, kpoint_of_pool):
    own = psi[0]
    grid = own.shape[2]
    half = half_width(grid)
    band_dev = own.shape[1]
    ring = lax.axis_size("band")
    block = band_dev * ring
    pools = lax.axis_size("kpool")
    myself = lax.axis_index("kpool")
    coords = kpoint_coords(kpoint_of_pool)
    here = lax.dynamic_index_in_dim(coords, myself, 0, keepdims=False)
    lower = lax.dynamic_index_in_dim(coords, (myself - 1) % pools, 0, keepdims=False)
    upper = lax.dynamic_index_in_dim(coords, (myself + 1) % pools, 0, keepdims=False)
    v_lower = coulomb(here - lower, grid)
    v_upper = coulomb(here - upper, grid)
    points = grid * grid
    parts = own.reshape(2, band_dev, points, grid)
    parts = jnp.pad(parts, ((0, 0), (0, 0), (0, 0), (0, half - grid)))
    packed = jnp.concatenate([parts[0], parts[1]], axis=-1)

    held = {0: packed}
    for step in range(1, ring):
        if step > 1 and step == ring - 1:
            held[step] = sent(packed, 0, -1)
        else:
            held[step] = sent(held[step - 1], 0, 1)
    steps = [0] + ([1] if ring > 1 else []) + list(range(ring - 1, 1, -1))
    accs = [None] * band_dev
    for step in steps:
        lower_bands = sent(held[step], 1, 0)
        upper_bands = sent(held[step], -1, 0)
        for n in range(band_dev):
            for m in range(band_dev):
                accs[n] = pair_sums(
                    packed[n],
                    [lower_bands[m], upper_bands[m]],
                    [v_lower, v_upper],
                    accs[n],
                    grid,
                )
    weight = -((2.0 * ROUNDS * block) ** (-0.5))
    total = jnp.stack(accs)
    total = total * weight
    result = jnp.stack([total[..., :grid], total[..., half : half + grid]])
    return result.reshape(2, band_dev, grid, grid * grid)[None]


def solution(mesh):
    in_specs = (P("kpool", None, "band", None, None), P())
    out_specs = P("kpool", None, "band", None, None)
    return jax.shard_map(
        per_device, mesh=mesh, in_specs=in_specs, out_specs=out_specs, check_vma=False
    )
```
